512 devices in a mesh: wave: 128 (over y_lo, z, x), parity: 2 (over y_hi), lev: 2 (over core).
Axes of the slice: x: 4, y: 4 (y_hi: 2, y_lo: 2; y = y_hi * 2 + y_lo), z: 16, core: 2. Of those that a mesh axis runs over, the one named last changes fastest.
Arguments:
- fourier: bfloat16 [2, 1280, 256, 256], P('parity', 'wave', None, 'lev'), may hold values from -6 to 6
- legendre: bfloat16 [256, 2, 1280, 1280], P('wave', 'parity', 'lev'), may hold values from -0.15625 to 0.15625
- quad_weights: float32 [1280], P('wave'), may hold values from 0.3 to 3
- slot_wave: int32 [256], replicated, may hold values from 0 to 255, as said below
- to_modes: float32 [128, 128], replicated, may hold values from -0.5 to 0.5
- from_modes: float32 [128, 128], replicated, may hold values from -0.5 to 0.5
- mode_rates: float32 [128], replicated, may hold values from 0.1 to 10
Outputs:
- columns: bfloat16 [2, 1280, 256, 256], P('parity', 'wave', None, 'lev')
- spectral: bfloat16 [2, 1280, 65536], P('parity', 'lev', 'wave')
The draws below stay inside these ranges and needn't reach their ends.
Inputs may be any that keep to these rules, and one draw needn't show every extreme that they name: `slot_wave`: A permutation of the wavenumbers 0 to 255; the owner with index w on wave holds slots w * 2 to (w + 1) * 2 - 1. Slots 2 i and 2 i + 1 hold a wavenumber below 128 and 255 minus it, in that order.
All inputs are finite; a program needn't handle non-finite values.
Results may differ from the reference program's by a relative error of at most 0.014.
Values may be sent and summed in bfloat16 or wider, within the bound.
A program may use at most 128 MiB of HBM per device.

```python
import math
import jax
import jax.numpy as jnp
from jax import lax

NLAT_H = 1280
NDEG_H = 1280
LEVELS = 128
M_DEV = 2
WAVES = 256


def draw_slot_wave(key, part):
    if M_DEV % 2 == 0:
        low_half = jax.random.permutation(key, WAVES // 2).astype(jnp.int32)
        return jnp.stack([low_half, WAVES - 1 - low_half], axis=1).reshape(-1).astype(jnp.int32)
    return jax.random.permutation(key, WAVES).astype(jnp.int32)


def shard_levels(key, extent, cuts, low, top_value):
    def one(dim, blocks):
        heights = jax.random.uniform(jax.random.fold_in(jax.random.fold_in(key, 6), dim), (blocks,), jnp.float32, low / len(cuts), top_value / len(cuts))
        return jnp.repeat(jnp.exp(heights), extent[dim] // blocks).reshape((-1,) + (1,) * (len(extent) - dim - 1))

    level = one(*cuts[0])
    for cut in cuts[1:]:
        level = level * one(*cut)
    return level


def bell_draw(rng, dims, spread, reach, pieces=(), held_as=jnp.bfloat16):
    result = spread * jax.random.normal(rng, dims, jnp.float32)
    if pieces:
        result = result * shard_levels(rng, dims, pieces, -0.22, 0.18)
    return jnp.clip(result, -reach, reach).astype(held_as)


def setup_inputs(seed: int = 0) -> dict:
    key_list = jax.random.split(jax.random.key(seed), 8)
    return {
        "fourier": bell_draw(key_list[0], (2, NLAT_H, WAVES, 2 * LEVELS), 1.0, 6.0, ((0, 2), (1, 128), (3, 2))),
        "legendre": bell_draw(key_list[1], (WAVES, 2, NLAT_H, NDEG_H), NLAT_H ** -0.5, 0.15625, ((0, 128), (1, 2), (2, 2))),
        "quad_weights": jnp.clip(jnp.exp(math.log(3.0) - 2.3025851 * jax.random.uniform(key_list[2], (NLAT_H,), jnp.float32) ** shard_levels(key_list[2], (NLAT_H,), ((0, 128),), -0.2, 0.2)), 0.3, 3.0),
        "slot_wave": draw_slot_wave(jax.random.fold_in(key_list[7], 71), 0),
        "to_modes": bell_draw(key_list[4], (LEVELS, LEVELS), LEVELS ** -0.5, 0.5, (), jnp.float32),
        "from_modes": bell_draw(key_list[5], (LEVELS, LEVELS), LEVELS ** -0.5, 0.5, (), jnp.float32),
        "mode_rates": jnp.clip(jnp.exp(jax.random.uniform(key_list[6], (LEVELS,), jnp.float32, math.log(0.1), math.log(10.0))), 0.1, 10.0),
    }


def reference(fourier, legendre, quad_weights, slot_wave, to_modes, from_modes, mode_rates):
    top_degree = 2 * NDEG_H - 1
    scaled = (quad_weights[None, :, None, None] * fourier.astype(jnp.float32)).astype(jnp.bfloat16)
    widened = scaled.astype(jnp.float32)
    folded = jnp.stack([widened[0] + widened[1], widened[0] - widened[1]]).astype(jnp.bfloat16)
    by_slot = jnp.moveaxis(jnp.take(folded, slot_wave, axis=2), 2, 0)
    parity_idx = jnp.arange(2, dtype=jnp.int32)
    degree_idx = jnp.arange(NDEG_H, dtype=jnp.int32)

    def per_slot(operands):
        rows_table, rows_data, wavenum = operands
        table_wide = rows_table.astype(jnp.float32)
        raw = jnp.einsum("qjk,qjc->qkc", table_wide, rows_data.astype(jnp.float32))
        degree = (wavenum + 2 * degree_idx[None, :] + parity_idx[:, None]).astype(jnp.int32)
        kept = jnp.where((degree <= top_degree)[:, :, None], raw, jnp.zeros_like(raw))
        shaped = kept.reshape(2, NDEG_H, LEVELS, 2)
        mode_part = jnp.einsum("il,qklr->qkir", to_modes, shaped, precision=lax.Precision.HIGHEST)
        degree_f = degree.astype(jnp.float32)
        stiffness = degree_f * (degree_f + 1.0) / (top_degree * (top_degree + 1.0))
        mode_part = mode_part / (1.0 + stiffness[:, :, None, None] * mode_rates[None, None, :, None])
        updated = jnp.einsum("li,qkir->qklr", from_modes, mode_part, precision=lax.Precision.HIGHEST)
        updated = updated.reshape(2, NDEG_H, 2 * LEVELS).astype(jnp.bfloat16)
        parts = jnp.einsum("qjk,qkc->qjc", table_wide, updated.astype(jnp.float32)).astype(jnp.bfloat16)
        return updated, parts

    updated_all, parts_all = lax.map(per_slot, (legendre, by_slot, slot_wave))
    wave_count = slot_wave.shape[0]
    spectral = jnp.transpose(updated_all, (1, 2, 0, 3)).reshape(2, NDEG_H, wave_count * 2 * LEVELS)
    wide_parts = parts_all.astype(jnp.float32)
    joined = jnp.stack([wide_parts[:, 0] + wide_parts[:, 1], wide_parts[:, 0] - wide_parts[:, 1]]).astype(jnp.bfloat16)
    inverse_slot = jnp.zeros((wave_count,), jnp.int32).at[slot_wave].set(jnp.arange(wave_count, dtype=jnp.int32))
    columns = jnp.transpose(jnp.take(joined, inverse_slot, axis=1), (0, 2, 1, 3))
    return columns, spectral
```

```python
import jax
import jax.numpy as jnp
from jax import lax
from jax.experimental import pallas as pl
from jax.experimental.pallas import tpu as pltpu
from jax.sharding import PartitionSpec as P

MESH = pl.DeviceIdType.MESH
F32 = jnp.float32
BF16 = jnp.bfloat16
NY, NZ, NX = 2, 16, 4
CORES = 2


def dot(a, b, dims=((1,), (0,)), precision=None):
    return lax.dot_general(a, b, (dims, ((), ())), precision=precision, preferred_element_type=F32)


def make_kernel(lats, waves, half, degrees):
    nlat = NY * NZ * NX * lats
    zlats = NX * lats
    side = nlat // 2
    width = 2 * half
    peers = NY * NX
    rows = waves // 2
    top = 2 * degrees - 1

    def kernel(
        fourier, legendre, quad_in, slots_in, slots_row, to_in, from_in, rates_in,
        columns, spectral,
        quad, slots_s, slots_v, to_modes, from_modes, rates,
        grid_in, send1, recv1, fold, send2, table_in, table, modes, picks, back,
        updated, parts, recv3, send4, recv4, turned, early,
        local_sem, small_sem, bar_leg, leg_send, spec_sem, spec_send, spec_recv,
        s1, r1, s2, r2, s3, r3, s4, r4, turn,
    ):
        w = lax.axis_index("wave")
        par = lax.axis_index("parity")
        lev = lax.axis_index("lev")
        yl = w // (NZ * NX)
        z = (w // NX) % NZ
        x = w % NX
        sign = (1 - 2 * par).astype(F32)

        def dev(y, zz, xx, q, l):
            return ((y * NZ + zz) * NX + xx, q, l)

        def is_me(d):
            return (d[0] == w) & (d[1] == par) & (d[2] == lev)

        def plane_dst(n):
            q = (par + 1 + n // 8) % 2
            y = (yl + (n // 4) % 2) % 2
            xx = (x + n) % NX
            return y, xx, dev(y, z, xx, q, yl)

        def plane_src(n, l):
            h = (par + 1 + n // NX) % 2
            xx = (x + n) % NX
            return xx, dev(lev, z, xx, h, l)

        def ring(t):
            mag = NZ // 2 - (t + 1) // 2
            return (z + (2 * (t % 2) - 1) * mag + NZ) % NZ

        def signal(d, sem):
            @pl.when(jnp.logical_not(is_me(d)))
            def _():
                pl.semaphore_signal(sem, inc=1, device_id=d, device_id_type=MESH)

        def post(src, dst, send_sem, recv_sem, d):
            me = is_me(d)

            @pl.when(jnp.logical_not(me))
            def _():
                pltpu.make_async_remote_copy(
                    src_ref=src, dst_ref=dst, send_sem=send_sem, recv_sem=recv_sem,
                    device_id=d, device_id_type=MESH,
                ).start()

            @pl.when(me)
            def _():
                pltpu.make_async_copy(src, dst, recv_sem).start()

        def await_bytes(ref, sem):
            pltpu.make_async_copy(ref, ref, sem).wait()

        get_grid = pltpu.make_async_copy(fourier.at[0], grid_in, local_sem.at[0])
        get_grid.start()
        get_leg = pltpu.make_async_copy(
            legendre.at[lev, 0], table.at[pl.ds(lev * side, side)], local_sem.at[1]
        )
        get_leg.start()

        small = [
            pltpu.make_async_copy(src, dst, small_sem.at[n])
            for n, (src, dst) in enumerate((
                (slots_row, slots_v), (quad_in, quad), (slots_in, slots_s),
                (to_in, to_modes), (from_in, from_modes), (rates_in, rates),
            ))
        ]
        for copy in small:
            copy.start()

        barrier = pltpu.get_barrier_semaphore()

        def greet_ring(n, _):
            signal(dev(yl, ring(n // 2), x, par, n % 2), barrier)
            return 0

        def greet_plane(n, _):
            signal(plane_dst(n)[2], barrier)
            signal(plane_src(n // 2, n % 2)[1], barrier)
            return 0

        lax.fori_loop(0, NZ * CORES, greet_ring, 0)
        lax.fori_loop(0, 2 * peers, greet_plane, 0)

        small[0].wait()
        small[1].wait()

        row = lax.broadcasted_iota(jnp.int32, (waves, waves), 0)
        col = lax.broadcasted_iota(jnp.int32, (waves, waves), 1)
        hot = (row == slots_v[...]).astype(F32).astype(BF16)
        zz = row & 15
        xx = (row >> 4) & 3
        yy = (row >> 6) & 1
        ii = row >> 7
        order = (col == (((yy * NZ + zz) * NX + xx) * 2 + ii)).astype(F32).astype(BF16)
        picks[...] = dot(order, hot, ((1,), (1,))).astype(BF16)

        get_grid.wait()
        for pair in range(lats // 2):
            two = [
                (quad[2 * pair + b] * grid_in[2 * pair + b].astype(F32)).astype(BF16)
                for b in range(2)
            ]
            moved = dot(picks[...], jnp.concatenate(two, axis=1)).astype(BF16)
            for i in range(2):
                for b in range(2):
                    block = moved[i * rows : (i + 1) * rows, b * half : (b + 1) * half]
                    send1[i, :, 2 * pair + b] = block.reshape(peers, NZ, half)

        different = (lev != yl).astype(jnp.int32)
        pl.semaphore_wait(barrier, 2 * (2 * peers - 1) + NZ * CORES - 1 + 2 * different)

        def go1(i, first, count, sem):
            def one(n, _):
                y, xx_, d = plane_dst(n)
                post(
                    send1.at[i, y * NX + xx_],
                    recv1.at[i, lev * peers + par * NX + x],
                    s1.at[sem], r1.at[i * 2 + lev], d,
                )
                return 0

            lax.fori_loop(first, first + count, one, 0)

        def pass_on():
            await_bytes(recv1.at[0, pl.ds(0, peers)], s1.at[0])
            pl.semaphore_signal(turn, inc=1, device_id=(w, par, 1 - lev), device_id_type=MESH)

        @pl.when(lev == 0)
        def _():
            go1(0, 0, peers, 0)
            go1(0, peers, peers, 1)
            pass_on()

        @pl.when(lev == 1)
        def _():
            pl.semaphore_wait(turn, 1)
            go1(0, 0, peers, 0)
            go1(0, peers, peers, 1)
            go1(1, 0, 2 * peers, 2)
            pass_on()

        swap = pltpu.make_async_remote_copy(
            src_ref=legendre.at[1 - lev, 0],
            dst_ref=table.at[pl.ds(lev * side, side)],
            send_sem=leg_send.at[0], recv_sem=bar_leg.at[0],
            device_id=(w, par, 1 - lev), device_id_type=MESH,
        )
        swap.start()

        for copy in small[2:]:
            copy.wait()

        into = dot(hot, order, ((1,), (1,)))
        for i in range(2):
            one = into[:, i * rows : (i + 1) * rows]
            back[:, (2 * i) * rows : (2 * i + 1) * rows] = one.astype(BF16)
            back[:, (2 * i + 1) * rows : (2 * i + 2) * rows] = (sign * one).astype(BF16)

        wide_l = lax.broadcasted_iota(jnp.int32, (width, half), 0) >> 1
        spread = (wide_l == lax.broadcasted_iota(jnp.int32, (width, half), 1)).astype(F32)
        same = ((row ^ col) & 1) == 0
        for index, square in enumerate((to_modes, from_modes)):
            tall = dot(spread, square[...], precision=lax.Precision.HIGHEST)
            full = dot(tall, spread, ((1,), (1,)), precision=lax.Precision.HIGHEST)
            modes[index] = jnp.where(same, full, 0.0)
        rates_col = jnp.sum(spread * rates[...], axis=1, keepdims=True)
        eye = (row == col).astype(F32).astype(BF16)

        for chunk in range(4):
            i, l = chunk // 2, chunk % 2
            await_bytes(recv1.at[i, pl.ds(l * peers, peers)], r1.at[chunk])
            for xs in range(NX):
                north = recv1[i, l * peers + xs].astype(F32)
                south = recv1[i, l * peers + NX + xs].astype(F32)
                both = (north + sign * south).reshape(lats * NZ, half)
                fold[xs * lats * NZ : (xs + 1) * lats * NZ, :] = both
            for t in range(NZ):
                send2[chunk, t] = fold[pl.ds(t, zlats, stride=NZ), :].astype(BF16)

            def go2(t, _):
                to = ring(t)
                post(
                    send2.at[chunk, to],
                    table_in.at[l, pl.ds(pl.multiple_of(lev * side + z * zlats, 8), zlats)],
                    s2.at[i], r2.at[l], dev(yl, to, x, par, i),
                )
                return 0

            lax.fori_loop(0, NZ, go2, 0)
            if chunk == 0:

                @pl.when(lev == 0)
                def _():
                    pl.semaphore_wait(turn, 1)
                    go1(1, 0, 2 * peers, 2)

        get_leg.wait()
        swap.wait_recv()
        for l in range(2):
            await_bytes(table_in.at[l], r2.at[l])
            for b in range(nlat // 256):
                turned[l * half : (l + 1) * half, b * 256 : (b + 1) * 256] = dot(
                    eye[:half, :half], table_in[l, b * 256 : (b + 1) * 256, :], ((1,), (1,))
                ).astype(BF16)
        wave = slots_s[2 * w + lev]

        def degrees_step(b, _):
            start = pl.multiple_of(b * 256, 256)
            raw = dot(turned[...], table[:, pl.ds(start, 256)])
            k = lax.broadcasted_iota(jnp.int32, (1, 256), 1) + start
            n = wave + 2 * k + par
            kept = jnp.where(n <= top, raw, 0.0)
            nf = n.astype(F32)
            stiff = nf * (nf + 1.0) / (top * (top + 1.0))
            modal = dot(modes[0], kept, precision=lax.Precision.HIGHEST)
            damped = modal / (1.0 + stiff * rates_col)
            new = dot(modes[1], damped, precision=lax.Precision.HIGHEST).astype(BF16)
            updated[pl.ds(start, 256), :] = dot(eye, new, ((1,), (1,))).astype(BF16)
            return 0

        lax.fori_loop(0, degrees // 256, degrees_step, 0)

        kept_half = degrees // 2
        lanes = pl.ds(pl.multiple_of(lev * width, width), width)
        put_spec = pltpu.make_async_copy(
            updated.at[pl.ds(lev * kept_half, kept_half)], spectral.at[0, :, lanes], spec_sem.at[0]
        )
        put_spec.start()

        def lats_step(b, _):
            start = pl.multiple_of(b * 256, 256)
            new = dot(table[pl.ds(start, 256), :], updated[...]).astype(BF16)
            for l in range(2):
                parts[l, pl.ds(start, 256), :] = new[:, l * half : (l + 1) * half]
            return 0

        lax.fori_loop(0, nlat // 256, lats_step, 0)

        for l in range(2):

            def go3(t, _):
                to = ring(t // 2)
                side_to = t % 2
                post(
                    parts.at[l, pl.ds(pl.multiple_of(side_to * side + to * zlats, 8), zlats)],
                    recv3.at[(lev * 2 + l) * NZ + z],
                    s3.at[0], r3.at[lev * 2 + l], dev(yl, to, x, par, side_to),
                )
                return 0

            lax.fori_loop(0, NZ * CORES, go3, 0)

        swap_spec = pltpu.make_async_remote_copy(
            src_ref=updated.at[pl.ds((1 - lev) * kept_half, kept_half)],
            dst_ref=spectral.at[0, :, lanes],
            send_sem=spec_send.at[0], recv_sem=spec_recv.at[0],
            device_id=(w, par, 1 - lev), device_id_type=MESH,
        )
        swap_spec.start()

        for chunk in range(4):
            i, l = chunk // 2, chunk % 2
            await_bytes(recv3.at[pl.ds(chunk * NZ, NZ)], r3.at[chunk])
            for t in range(NZ):
                fold[t * zlats : (t + 1) * zlats, :] = recv3[chunk * NZ + t].astype(F32)
            for lat in range(zlats):
                picked = fold[pl.ds(lat, NZ, stride=zlats), :]
                send4[chunk, lat // lats, lat % lats] = picked.astype(BF16)

            def go4(n, _):
                xx_, d = plane_src(n, l)
                post(
                    send4.at[chunk, xx_], recv4.at[i, par * peers + yl * NX + x],
                    s4.at[i], r4.at[i], d,
                )
                return 0

            lax.fori_loop(0, peers, go4, 0)

        for i in range(2):
            await_bytes(recv4.at[i], r4.at[i])
            for pair in range(lats // 2):
                cols = [recv4[i, :, 2 * pair + b].reshape(2 * rows, half) for b in range(2)]
                share = dot(
                    back[:, 2 * i * rows : 2 * (i + 1) * rows], jnp.concatenate(cols, axis=1)
                )
                if i == 0:
                    early[pair] = share
                else:
                    both = (early[pair] + share).astype(BF16)
                    for b in range(2):
                        columns[0, 2 * pair + b] = both[:, b * half : (b + 1) * half]

        swap.wait_send()
        swap_spec.wait()
        put_spec.wait()
        await_bytes(recv3.at[pl.ds(0, 2 * NZ * CORES - 2)], s3.at[0])

        def drain(ref, count, sem, has_local):
            @pl.when(has_local)
            def _():
                await_bytes(ref.at[pl.ds(0, count - 1)], sem)

            @pl.when(jnp.logical_not(has_local))
            def _():
                await_bytes(ref.at[pl.ds(0, count)], sem)

        local = lev == yl
        drain(recv1.at[0], peers, s1.at[1], local)
        drain(recv1.at[1], 2 * peers, s1.at[2], local)
        for i in range(2):
            drain(recv4.at[i], 2 * peers, s4.at[i], local)

            @pl.when(lev == i)
            def _():
                await_bytes(recv3.at[pl.ds(0, 2 * NZ - 2)], s2.at[i])

            @pl.when(lev != i)
            def _():
                await_bytes(recv3.at[pl.ds(0, 2 * NZ)], s2.at[i])

    scratch = [
        pltpu.SMEM((lats,), F32),
        pltpu.SMEM((waves,), jnp.int32),
        pltpu.VMEM((1, waves), jnp.int32),
        pltpu.VMEM((half, half), F32),
        pltpu.VMEM((half, half), F32),
        pltpu.VMEM((1, half), F32),
        pltpu.VMEM((lats, waves, half), BF16),
        pltpu.VMEM((2, peers, lats, NZ, half), BF16),
        pltpu.VMEM((2, 2 * peers, lats, NZ, half), BF16),
        pltpu.VMEM((zlats * NZ, half), F32),
        pltpu.VMEM((4, NZ, zlats, half), BF16),
        pltpu.VMEM((2, nlat, half), BF16),
        pltpu.VMEM((nlat, degrees), BF16),
        pltpu.VMEM((2, width, width), F32),
        pltpu.VMEM((waves, waves), BF16),
        pltpu.VMEM((waves, 2 * waves), BF16),
        pltpu.VMEM((degrees, width), BF16),
        pltpu.VMEM((2, nlat, half), BF16),
        pltpu.VMEM((4 * NZ, zlats, half), BF16),
        pltpu.VMEM((4, NX, lats, NZ, half), BF16),
        pltpu.VMEM((2, 2 * peers, lats, NZ, half), BF16),
        pltpu.VMEM((width, nlat), BF16),
        pltpu.VMEM((lats // 2, waves, 2 * half), F32),
        pltpu.SemaphoreType.DMA((2,)),
        pltpu.SemaphoreType.DMA((6,)),
    ] + [pltpu.SemaphoreType.DMA((1,))] * 5 + [
        pltpu.SemaphoreType.DMA((3,)),
        pltpu.SemaphoreType.DMA((4,)),
        pltpu.SemaphoreType.DMA((2,)),
        pltpu.SemaphoreType.DMA((2,)),
        pltpu.SemaphoreType.DMA((1,)),
        pltpu.SemaphoreType.DMA((4,)),
        pltpu.SemaphoreType.DMA((2,)),
        pltpu.SemaphoreType.DMA((2,)),
        pltpu.SemaphoreType.REGULAR,
    ]
    return kernel, scratch


def per_device(fourier, legendre, quad_weights, slot_wave, to_modes, from_modes, mode_rates):
    _, lats, waves, half = fourier.shape
    degrees = legendre.shape[3]
    kernel, scratch = make_kernel(lats, waves, half, degrees)
    vmem = pl.BlockSpec(memory_space=pltpu.VMEM)
    hbm = pl.BlockSpec(memory_space=pltpu.HBM)
    operands = (
        fourier, legendre, quad_weights, slot_wave, slot_wave.reshape(1, waves),
        to_modes, from_modes, mode_rates.reshape(1, half),
    )
    return pl.pallas_call(
        kernel,
        out_shape=(
            jax.ShapeDtypeStruct(fourier.shape, BF16),
            jax.ShapeDtypeStruct((1, degrees // 2, 2 * 2 * half), BF16),
        ),
        in_specs=[hbm] * 8,
        out_specs=(vmem, vmem),
        scratch_shapes=scratch,
        compiler_params=pltpu.CompilerParams(
            collective_id=0, has_side_effects=True, vmem_limit_bytes=48 * 2**20
        ),
    )(*[pltpu.with_memory_space_constraint(v, pltpu.HBM) for v in operands])


def solution(mesh):
    in_specs = (
        P("parity", "wave", None, "lev"),
        P("wave", "parity", "lev", None),
        P("wave"),
        P(),
        P(),
        P(),
        P(),
    )
    out_specs = (P("parity", "wave", None, "lev"), P("parity", "lev", "wave"))
    return jax.shard_map(
        per_device, mesh=mesh, in_specs=in_specs, out_specs=out_specs, check_vma=False
    )
```

```python
import jax
import jax.numpy as jnp
from jax import lax
from jax.experimental import pallas as pl
from jax.experimental.pallas import tpu as pltpu
from jax.sharding import PartitionSpec as P

MESH = pl.DeviceIdType.MESH
F32 = jnp.float32
BF16 = jnp.bfloat16
NY, NZ, NX = 2, 16, 4
CORES = 2


def dot(a, b, dims=((1,), (0,)), precision=None):
    return lax.dot_general(a, b, (dims, ((), ())), precision=precision, preferred_element_type=F32)


def make_kernel(lats, waves, half, degrees):
    nlat = NY * NZ * NX * lats
    zlats = NX * lats
    side = nlat // 2
    width = 2 * half
    peers = NY * NX
    rows = waves // 2
    top = 2 * degrees - 1

    def kernel(
        fourier, legendre, quad_in, slots_in, slots_row, to_in, from_in, rates_in,
        columns, spectral,
        quad, slots_s, slots_v, to_modes, from_modes, rates,
        grid_in, send1, recv1, fold, send2, table_in, table, modes, picks, back,
        updated, parts, recv3, send4, recv4, turned, early,
        local_sem, small_sem, bar_leg, leg_send, spec_sem, spec_send, spec_recv,
        s1, r1, s2, r2, s3, r3, s4, r4, turn, known, told,
    ):
        w = lax.axis_index("wave")
        par = lax.axis_index("parity")
        lev = lax.axis_index("lev")
        yl = w >> 6
        z = (w >> 2) & 15
        x = w & 3
        local = lev == yl
        sign = (1 - 2 * par).astype(F32)

        def dev(y, zz, xx, q, l):
            return ((y << 6) + (zz << 2) + xx, q, l)

        def plane_dst(n):
            q = (par + 1 + (n >> 3)) & 1
            y = (yl + (n >> 2)) & 1
            xx = (x + n) & 3
            return (y << 2) + xx, dev(y, z, xx, q, yl)

        def plane_src(n, l):
            h = (par + 1 + (n >> 2)) & 1
            xx = (x + n) & 3
            return xx, dev(lev, z, xx, h, l)

        def ring(t):
            away = ((t + 1) >> 1) * (2 * (t & 1) - 1)
            return (z + 8 + away) & 15

        def signal(d, sem):
            pl.semaphore_signal(sem, inc=1, device_id=d, device_id_type=MESH)

        def send(src, dst, send_sem, recv_sem, d):
            pltpu.make_async_remote_copy(
                src_ref=src, dst_ref=dst, send_sem=send_sem, recv_sem=recv_sem,
                device_id=d, device_id_type=MESH,
            ).start()

        def post(me, src, dst, send_sem, recv_sem, d):
            @pl.when(jnp.logical_not(me))
            def _():
                send(src, dst, send_sem, recv_sem, d)

            @pl.when(me)
            def _():
                pltpu.make_async_copy(src, dst, recv_sem).start()

        def loop(first, last, body):
            def step(n, _):
                body(n)
                return 0

            lax.fori_loop(first, last, step, 0)

        def await_bytes(ref, sem):
            pltpu.make_async_copy(ref, ref, sem).wait()

        get_grid = pltpu.make_async_copy(fourier.at[0], grid_in, local_sem.at[0])
        get_grid.start()
        small = [
            pltpu.make_async_copy(src, dst, small_sem.at[n])
            for n, (src, dst) in enumerate((
                (slots_row, slots_v), (quad_in, quad), (slots_in, slots_s),
                (to_in, to_modes), (from_in, from_modes), (rates_in, rates),
            ))
        ]
        for copy in small[:2]:
            copy.start()

        barrier = pltpu.get_barrier_semaphore()

        def tell(away, sem):
            for side_to in (-away, away):
                signal(dev(yl, (z + side_to) & 15, x, par, 0), sem)

        tell(1, barrier)

        def greet_dst(n):
            signal(plane_dst(n)[1], barrier)

        def greet_src(n):
            for l in range(2):
                signal(plane_src(n, l)[1], barrier)

        loop(0, 8, greet_dst)
        loop(9, 16, greet_dst)
        loop(0, 4, greet_src)
        loop(5, 8, greet_src)
        signal((w, par, 1 - lev), barrier)
        signal(plane_src(4, 1 - lev)[1], barrier)

        @pl.when(jnp.logical_not(local))
        def _():
            signal(plane_dst(8)[1], barrier)
            signal(plane_src(4, lev)[1], barrier)

        get_leg = pltpu.make_async_copy(
            legendre.at[lev, 0], table.at[pl.ds(lev * side, side)], local_sem.at[1]
        )
        get_leg.start()
        for copy in small[2:]:
            copy.start()

        small[0].wait()
        small[1].wait()

        row = lax.broadcasted_iota(jnp.int32, (waves, waves), 0)
        col = lax.broadcasted_iota(jnp.int32, (waves, waves), 1)
        hot = (row == slots_v[...]).astype(F32).astype(BF16)
        zz = row & 15
        xx = (row >> 4) & 3
        yy = (row >> 6) & 1
        ii = row >> 7
        order = (col == (((yy * NZ + zz) * NX + xx) * 2 + ii)).astype(F32).astype(BF16)
        picks[...] = dot(order, hot, ((1,), (1,))).astype(BF16)

        def permute(i):
            for pair in range(lats // 2):
                both = jnp.concatenate([grid_in[2 * pair + b] for b in range(2)], axis=1)
                moved = dot(picks[i * rows : (i + 1) * rows, :], both).astype(BF16)
                for b in range(2):
                    block = moved[:, b * half : (b + 1) * half]
                    send1[i, :, 2 * pair + b] = block.reshape(peers, NZ, half)

        get_grid.wait()
        for lat in range(lats):
            grid_in[lat] = (quad[lat] * grid_in[lat].astype(F32)).astype(BF16)
        permute(0)

        different = (lev != yl).astype(jnp.int32)
        first = (lev == 0).astype(jnp.int32)
        pl.semaphore_wait(barrier, 2 * (2 * peers - 1) + 1 + 2 * different + 4 * first)

        def go1(i, far, near):
            def parts_of(n):
                p, d = plane_dst(n)
                return send1.at[i, p], recv1.at[i, lev * peers + par * NX + x], d

            def one(sem):
                def body(n):
                    src, dst, d = parts_of(n)
                    send(src, dst, s1.at[sem], r1.at[i * 2 + lev], d)

                return body

            loop(0, 8, one(far))
            loop(9, 16, one(near))
            src, dst, d = parts_of(8)
            post(local, src, dst, s1.at[near], r1.at[i * 2 + lev], d)

        def pass_on():
            await_bytes(recv1.at[0, pl.ds(0, peers)], s1.at[0])
            signal((w, par, 1 - lev), turn)

        @pl.when(lev == 0)
        def _():
            tell(1, known.at[0])
            go1(0, 0, 1)
            pl.semaphore_wait(known.at[0], 2)
            tell(2, known.at[1])

        permute(1)

        @pl.when(lev == 0)
        def _():
            pass_on()
            pl.semaphore_wait(known.at[1], 2)
            tell(4, known.at[2])
            pl.semaphore_wait(known.at[2], 2)
            signal((w, par, 1), told)

        @pl.when(lev == 1)
        def _():
            pl.semaphore_wait(turn, 1)
            go1(0, 0, 1)
            go1(1, 2, 2)
            pass_on()

        swap = pltpu.make_async_remote_copy(
            src_ref=legendre.at[1 - lev, 0],
            dst_ref=table.at[pl.ds(lev * side, side)],
            send_sem=leg_send.at[0], recv_sem=bar_leg.at[0],
            device_id=(w, par, 1 - lev), device_id_type=MESH,
        )
        swap.start()

        for copy in small[2:]:
            copy.wait()

        into = dot(hot, order, ((1,), (1,)))
        for i in range(2):
            one = into[:, i * rows : (i + 1) * rows]
            back[:, (2 * i) * rows : (2 * i + 1) * rows] = one.astype(BF16)
            back[:, (2 * i + 1) * rows : (2 * i + 2) * rows] = (sign * one).astype(BF16)

        wide_l = lax.broadcasted_iota(jnp.int32, (width, half), 0) >> 1
        spread = (wide_l == lax.broadcasted_iota(jnp.int32, (width, half), 1)).astype(F32)
        same = ((row ^ col) & 1) == 0
        for index, square in enumerate((to_modes, from_modes)):
            tall = dot(spread, square[...], precision=lax.Precision.HIGHEST)
            full = dot(tall, spread, ((1,), (1,)), precision=lax.Precision.HIGHEST)
            full = jnp.where(same, full, 0.0)
            high = full.astype(BF16)
            low = (full - high.astype(F32)).astype(BF16)
            modes[index] = jnp.concatenate([high, high, low], axis=1)
        rates_col = jnp.sum(spread * rates[...], axis=1, keepdims=True)
        eye = (row == col).astype(F32).astype(BF16)

        for chunk in range(4):
            i, l = chunk // 2, chunk % 2
            await_bytes(recv1.at[i, pl.ds(l * peers, peers)], r1.at[chunk])
            for xs in range(NX):
                north = recv1[i, l * peers + xs].astype(F32)
                south = recv1[i, l * peers + NX + xs].astype(F32)
                both = (north + sign * south).reshape(lats * NZ, half)
                fold[xs * lats * NZ : (xs + 1) * lats * NZ, :] = both
            for t in range(NZ):
                send2[chunk, t] = fold[pl.ds(t, zlats, stride=NZ), :].astype(BF16)

            if chunk == 0:

                @pl.when(lev == 1)
                def _():
                    pl.semaphore_wait(told, 1)

            mine = pl.ds(pl.multiple_of(lev * side + z * zlats, 8), zlats)

            def go2(t):
                to = ring(t)
                send(
                    send2.at[chunk, to], table_in.at[l, mine], s2.at[i], r2.at[l],
                    dev(yl, to, x, par, i),
                )

            loop(0, NZ - 1, go2)
            post(
                lev == i, send2.at[chunk, z], table_in.at[l, mine], s2.at[i], r2.at[l],
                (w, par, i),
            )
            if chunk == 0:

                @pl.when(lev == 0)
                def _():
                    pl.semaphore_wait(turn, 1)
                    go1(1, 2, 2)

        get_leg.wait()
        swap.wait_recv()
        for l in range(2):
            await_bytes(table_in.at[l], r2.at[l])
            for b in range(nlat // 256):
                turned[l * half : (l + 1) * half, b * 256 : (b + 1) * 256] = dot(
                    eye[:half, :half], table_in[l, b * 256 : (b + 1) * 256, :], ((1,), (1,))
                ).astype(BF16)
        wave = slots_s[2 * w + lev]

        def mix(index, value):
            high = value.astype(BF16)
            low = (value - high.astype(F32)).astype(BF16)
            return dot(modes[index], jnp.concatenate([high, low, high], axis=0))

        for start in range(0, degrees, 256):
            raw = dot(turned[...], table[:, start : start + 256])
            k = lax.broadcasted_iota(jnp.int32, (1, 256), 1) + start
            n = wave + 2 * k + par
            kept = jnp.where(n <= top, raw, 0.0)
            nf = n.astype(F32)
            stiff = nf * (nf + 1.0) / (top * (top + 1.0))
            damped = mix(0, kept) / (1.0 + stiff * rates_col)
            new = mix(1, damped).astype(BF16)
            updated[start : start + 256, :] = dot(eye, new, ((1,), (1,))).astype(BF16)

        kept_half = degrees // 2
        lanes = pl.ds(pl.multiple_of(lev * width, width), width)
        put_spec = pltpu.make_async_copy(
            updated.at[pl.ds(lev * kept_half, kept_half)], spectral.at[0, :, lanes], spec_sem.at[0]
        )
        put_spec.start()

        for start in range(0, nlat, 256):
            new = dot(table[start : start + 256, :], updated[...]).astype(BF16)
            for l in range(2):
                parts[l, start : start + 256, :] = new[:, l * half : (l + 1) * half]

        for l in range(2):

            here = (lev * 2 + l) * NZ + z

            def rows_of(y, zz):
                return parts.at[l, pl.ds(pl.multiple_of(y * side + zz * zlats, 8), zlats)]

            def go3(t):
                to = ring(t)
                for y in range(2):
                    send(
                        rows_of(y, to), recv3.at[here], s3.at[0], r3.at[lev * 2 + l],
                        dev(yl, to, x, par, y),
                    )

            loop(0, NZ - 1, go3)
            send(
                rows_of(1 - lev, z), recv3.at[here], s3.at[0], r3.at[lev * 2 + l],
                (w, par, 1 - lev),
            )
            pltpu.make_async_copy(rows_of(lev, z), recv3.at[here], r3.at[lev * 2 + l]).start()

        swap_spec = pltpu.make_async_remote_copy(
            src_ref=updated.at[pl.ds((1 - lev) * kept_half, kept_half)],
            dst_ref=spectral.at[0, :, lanes],
            send_sem=spec_send.at[0], recv_sem=spec_recv.at[0],
            device_id=(w, par, 1 - lev), device_id_type=MESH,
        )
        swap_spec.start()

        for chunk in range(4):
            i, l = chunk // 2, chunk % 2
            await_bytes(recv3.at[pl.ds(chunk * NZ, NZ)], r3.at[chunk])
            for t in range(NZ):
                fold[t * zlats : (t + 1) * zlats, :] = recv3[chunk * NZ + t].astype(F32)
            for lat in range(zlats):
                picked = fold[pl.ds(lat, NZ, stride=zlats), :]
                send4[chunk, lat // lats, lat % lats] = picked.astype(BF16)

            def go4(n):
                xx, d = plane_src(n, l)
                send(
                    send4.at[chunk, xx], recv4.at[i, par * peers + (yl << 2) + x],
                    s4.at[i], r4.at[i], d,
                )

            loop(0, 4, go4)
            loop(5, 8, go4)
            xx, d = plane_src(4, l)
            post(
                local & (lev == l), send4.at[chunk, xx],
                recv4.at[i, par * peers + (yl << 2) + x], s4.at[i], r4.at[i], d,
            )

        for i in range(2):
            await_bytes(recv4.at[i], r4.at[i])
            for pair in range(lats // 2):
                cols = [recv4[i, :, 2 * pair + b].reshape(2 * rows, half) for b in range(2)]
                share = dot(
                    back[:, 2 * i * rows : 2 * (i + 1) * rows], jnp.concatenate(cols, axis=1)
                )
                if i == 0:
                    early[pair] = share
                else:
                    both = (early[pair] + share).astype(BF16)
                    for b in range(2):
                        columns[0, 2 * pair + b] = both[:, b * half : (b + 1) * half]

        swap.wait_send()
        swap_spec.wait()
        put_spec.wait()
        await_bytes(recv3.at[pl.ds(0, 2 * NZ * CORES - 2)], s3.at[0])

        def drain(ref, count, sem, has_local):
            @pl.when(has_local)
            def _():
                await_bytes(ref.at[pl.ds(0, count - 1)], sem)

            @pl.when(jnp.logical_not(has_local))
            def _():
                await_bytes(ref.at[pl.ds(0, count)], sem)

        drain(recv1.at[0], peers, s1.at[1], local)
        drain(recv1.at[1], 2 * peers, s1.at[2], local)
        for i in range(2):
            drain(recv4.at[i], 2 * peers, s4.at[i], local)

            @pl.when(lev == i)
            def _():
                await_bytes(recv3.at[pl.ds(0, 2 * NZ - 2)], s2.at[i])

            @pl.when(lev != i)
            def _():
                await_bytes(recv3.at[pl.ds(0, 2 * NZ)], s2.at[i])

    scratch = [
        pltpu.SMEM((lats,), F32),
        pltpu.SMEM((waves,), jnp.int32),
        pltpu.VMEM((1, waves), jnp.int32),
        pltpu.VMEM((half, half), F32),
        pltpu.VMEM((half, half), F32),
        pltpu.VMEM((1, half), F32),
        pltpu.VMEM((lats, waves, half), BF16),
        pltpu.VMEM((2, peers, lats, NZ, half), BF16),
        pltpu.VMEM((2, 2 * peers, lats, NZ, half), BF16),
        pltpu.VMEM((zlats * NZ, half), F32),
        pltpu.VMEM((4, NZ, zlats, half), BF16),
        pltpu.VMEM((2, nlat, half), BF16),
        pltpu.VMEM((nlat, degrees), BF16),
        pltpu.VMEM((2, width, 3 * width), BF16),
        pltpu.VMEM((waves, waves), BF16),
        pltpu.VMEM((waves, 2 * waves), BF16),
        pltpu.VMEM((degrees, width), BF16),
        pltpu.VMEM((2, nlat, half), BF16),
        pltpu.VMEM((4 * NZ, zlats, half), BF16),
        pltpu.VMEM((4, NX, lats, NZ, half), BF16),
        pltpu.VMEM((2, 2 * peers, lats, NZ, half), BF16),
        pltpu.VMEM((width, nlat), BF16),
        pltpu.VMEM((lats // 2, waves, 2 * half), F32),
        pltpu.SemaphoreType.DMA((2,)),
        pltpu.SemaphoreType.DMA((6,)),
    ] + [pltpu.SemaphoreType.DMA((1,))] * 5 + [
        pltpu.SemaphoreType.DMA((3,)),
        pltpu.SemaphoreType.DMA((4,)),
        pltpu.SemaphoreType.DMA((2,)),
        pltpu.SemaphoreType.DMA((2,)),
        pltpu.SemaphoreType.DMA((1,)),
        pltpu.SemaphoreType.DMA((4,)),
        pltpu.SemaphoreType.DMA((2,)),
        pltpu.SemaphoreType.DMA((2,)),
        pltpu.SemaphoreType.REGULAR,
        pltpu.SemaphoreType.REGULAR((3,)),
        pltpu.SemaphoreType.REGULAR,
    ]
    return kernel, scratch


def per_device(fourier, legendre, quad_weights, slot_wave, to_modes, from_modes, mode_rates):
    _, lats, waves, half = fourier.shape
    degrees = legendre.shape[3]
    kernel, scratch = make_kernel(lats, waves, half, degrees)
    vmem = pl.BlockSpec(memory_space=pltpu.VMEM)
    hbm = pl.BlockSpec(memory_space=pltpu.HBM)
    operands = (
        fourier, legendre, quad_weights, slot_wave, slot_wave.reshape(1, waves),
        to_modes, from_modes, mode_rates.reshape(1, half),
    )
    return pl.pallas_call(
        kernel,
        out_shape=(
            jax.ShapeDtypeStruct(fourier.shape, BF16),
            jax.ShapeDtypeStruct((1, degrees // 2, 2 * 2 * half), BF16),
        ),
        in_specs=[hbm] * 8,
        out_specs=(vmem, vmem),
        scratch_shapes=scratch,
        compiler_params=pltpu.CompilerParams(
            collective_id=0, has_side_effects=True, vmem_limit_bytes=48 * 2**20
        ),
    )(*[pltpu.with_memory_space_constraint(v, pltpu.HBM) for v in operands])


def solution(mesh):
    in_specs = (
        P("parity", "wave", None, "lev"),
        P("wave", "parity", "lev", None),
        P("wave"),
        P(),
        P(),
        P(),
        P(),
    )
    out_specs = (P("parity", "wave", None, "lev"), P("parity", "lev", "wave"))
    return jax.shard_map(
        per_device, mesh=mesh, in_specs=in_specs, out_specs=out_specs, check_vma=False
    )
```

```python
import jax
import jax.numpy as jnp
from jax import lax
from jax.experimental import pallas as pl
from jax.experimental.pallas import tpu as pltpu
from jax.sharding import PartitionSpec as P

MESH = pl.DeviceIdType.MESH
F32 = jnp.float32
BF16 = jnp.bfloat16
NY, NZ, NX = 2, 16, 4
CORES = 2


def dot(a, b, dims=((1,), (0,)), precision=None):
    return lax.dot_general(a, b, (dims, ((), ())), precision=precision, preferred_element_type=F32)


def make_kernel(lats, waves, half, degrees):
    nlat = NY * NZ * NX * lats
    zlats = NX * lats
    side = nlat // 2
    width = 2 * half
    peers = NY * NX
    rows = waves // 2
    top = 2 * degrees - 1

    def kernel(
        fourier, legendre, quad_in, slots_in, slots_row, to_in, from_in, rates_in,
        columns, spectral,
        quad, slots_s, slots_v, to_modes, from_modes, rates,
        grid_in, send1, recv1, fold, send2, table_in, table, modes, picks, back,
        updated, parts, recv3, send4, recv4, turned, early,
        local_sem, small_sem, bar_leg, leg_send, spec_sem, spec_send, spec_recv,
        s1, r1, s2, r2, s3, r3, s4, r4, turn, known, told,
    ):
        w = lax.axis_index("wave")
        par = lax.axis_index("parity")
        lev = lax.axis_index("lev")
        yl = w >> 6
        z = (w >> 2) & 15
        x = w & 3
        local = lev == yl
        sign = (1 - 2 * par).astype(F32)

        def dev(y, zz, xx, q, l):
            return ((y << 6) + (zz << 2) + xx, q, l)

        def plane_dst(n):
            q = (par + 1 + (n >> 3)) & 1
            y = (yl + (n >> 2)) & 1
            xx = (x + n * (1 - 2 * lev)) & 3
            return (y << 2) + xx, dev(y, z, xx, q, yl)

        def plane_src(n, l):
            h = (par + 1 + (n >> 2)) & 1
            xx = (x + n * (1 - 2 * lev)) & 3
            return xx, dev(lev, z, xx, h, l)

        def ring(t):
            away = ((t + 1) >> 1) * ((2 * (t & 1) - 1) * (1 - 2 * lev))
            return (z + 8 + away) & 15

        def signal(d, sem):
            pl.semaphore_signal(sem, inc=1, device_id=d, device_id_type=MESH)

        def send(src, dst, send_sem, recv_sem, d):
            pltpu.make_async_remote_copy(
                src_ref=src, dst_ref=dst, send_sem=send_sem, recv_sem=recv_sem,
                device_id=d, device_id_type=MESH,
            ).start()

        def post(me, src, dst, send_sem, recv_sem, d):
            @pl.when(jnp.logical_not(me))
            def _():
                send(src, dst, send_sem, recv_sem, d)

            @pl.when(me)
            def _():
                pltpu.make_async_copy(src, dst, recv_sem).start()

        def loop(first, last, body):
            def step(n, _):
                body(n)
                return 0

            lax.fori_loop(first, last, step, 0)

        def await_bytes(ref, sem):
            pltpu.make_async_copy(ref, ref, sem).wait()

        get_grid = pltpu.make_async_copy(fourier.at[0], grid_in, local_sem.at[0])
        get_grid.start()
        small = [
            pltpu.make_async_copy(src, dst, small_sem.at[n])
            for n, (src, dst) in enumerate((
                (slots_row, slots_v), (quad_in, quad), (slots_in, slots_s),
                (to_in, to_modes), (from_in, from_modes), (rates_in, rates),
            ))
        ]
        for copy in small[:2]:
            copy.start()

        barrier = pltpu.get_barrier_semaphore()

        def tell(away, sem):
            for side_to in (-away, away):
                signal(dev(yl, (z + side_to) & 15, x, par, 0), sem)

        tell(1, barrier)
        tell(2, barrier)

        def greet_dst(n):
            signal(plane_dst(n)[1], barrier)

        def greet_src(n):
            for l in range(2):
                signal(plane_src(n, l)[1], barrier)

        loop(0, 8, greet_dst)
        loop(9, 16, greet_dst)
        loop(0, 4, greet_src)
        loop(5, 8, greet_src)
        signal((w, par, 1 - lev), barrier)
        signal(plane_src(4, 1 - lev)[1], barrier)

        @pl.when(jnp.logical_not(local))
        def _():
            signal(plane_dst(8)[1], barrier)
            signal(plane_src(4, lev)[1], barrier)

        get_leg = pltpu.make_async_copy(
            legendre.at[lev, 0], table.at[pl.ds(lev * side, side)], local_sem.at[1]
        )
        get_leg.start()
        for copy in small[2:]:
            copy.start()

        small[0].wait()
        small[1].wait()

        row = lax.broadcasted_iota(jnp.int32, (waves, waves), 0)
        col = lax.broadcasted_iota(jnp.int32, (waves, waves), 1)
        hot = (row == slots_v[...]).astype(F32).astype(BF16)
        zz = row & 15
        xx = (row >> 4) & 3
        yy = (row >> 6) & 1
        ii = row >> 7
        order = (col == (((yy * NZ + zz) * NX + xx) * 2 + ii)).astype(F32).astype(BF16)
        picks[...] = dot(order, hot, ((1,), (1,))).astype(BF16)

        def permute(i):
            for pair in range(lats // 2):
                both = jnp.concatenate([grid_in[2 * pair + b] for b in range(2)], axis=1)
                moved = dot(picks[i * rows : (i + 1) * rows, :], both).astype(BF16)
                for b in range(2):
                    block = moved[:, b * half : (b + 1) * half]
                    send1[i, :, 2 * pair + b] = block.reshape(peers, NZ, half)

        get_grid.wait()
        for lat in range(lats):
            grid_in[lat] = (quad[lat] * grid_in[lat].astype(F32)).astype(BF16)
        permute(0)

        different = (lev != yl).astype(jnp.int32)
        first = (lev == 0).astype(jnp.int32)
        pl.semaphore_wait(barrier, 2 * (2 * peers - 1) + 1 + 2 * different + 8 * first)

        def go1(i, far, near):
            def parts_of(n):
                p, d = plane_dst(n)
                return send1.at[i, p], recv1.at[i, lev * peers + par * NX + x], d

            def one(sem):
                def body(n):
                    src, dst, d = parts_of(n)
                    send(src, dst, s1.at[sem], r1.at[i * 2 + lev], d)

                return body

            loop(0, 8, one(far))
            loop(9, 16, one(near))
            src, dst, d = parts_of(8)
            post(local, src, dst, s1.at[near], r1.at[i * 2 + lev], d)

        def pass_on():
            await_bytes(recv1.at[0, pl.ds(0, peers)], s1.at[0])
            signal((w, par, 1 - lev), turn)

        @pl.when(lev == 0)
        def _():
            tell(2, known.at[0])
            go1(0, 0, 1)
            pl.semaphore_wait(known.at[0], 2)
            tell(4, known.at[1])

        permute(1)

        @pl.when(lev == 0)
        def _():
            pass_on()
            pl.semaphore_wait(known.at[1], 2)
            signal((w, par, 1), told)

        @pl.when(lev == 1)
        def _():
            pl.semaphore_wait(turn, 1)
            go1(0, 0, 1)
            go1(1, 2, 2)
            pass_on()

        swap = pltpu.make_async_remote_copy(
            src_ref=legendre.at[1 - lev, 0],
            dst_ref=table.at[pl.ds(lev * side, side)],
            send_sem=leg_send.at[0], recv_sem=bar_leg.at[0],
            device_id=(w, par, 1 - lev), device_id_type=MESH,
        )
        swap.start()

        for copy in small[2:]:
            copy.wait()

        into = dot(hot, order, ((1,), (1,)))
        for i in range(2):
            one = into[:, i * rows : (i + 1) * rows]
            back[:, (2 * i) * rows : (2 * i + 1) * rows] = one.astype(BF16)
            back[:, (2 * i + 1) * rows : (2 * i + 2) * rows] = (sign * one).astype(BF16)

        wide_l = lax.broadcasted_iota(jnp.int32, (width, half), 0) >> 1
        spread = (wide_l == lax.broadcasted_iota(jnp.int32, (width, half), 1)).astype(F32)
        same = ((row ^ col) & 1) == 0
        for index, square in enumerate((to_modes, from_modes)):
            tall = dot(spread, square[...], precision=lax.Precision.HIGHEST)
            full = dot(tall, spread, ((1,), (1,)), precision=lax.Precision.HIGHEST)
            full = jnp.where(same, full, 0.0)
            high = full.astype(BF16)
            low = (full - high.astype(F32)).astype(BF16)
            modes[index] = jnp.concatenate([high, high, low], axis=1)
        rates_col = jnp.sum(spread * rates[...], axis=1, keepdims=True)
        eye = (row == col).astype(F32).astype(BF16)

        for chunk in range(4):
            i, l = chunk // 2, chunk % 2
            await_bytes(recv1.at[i, pl.ds(l * peers, peers)], r1.at[chunk])
            for xs in range(NX):
                north = recv1[i, l * peers + xs].astype(F32)
                south = recv1[i, l * peers + NX + xs].astype(F32)
                both = (north + sign * south).reshape(lats * NZ, half)
                fold[xs * lats * NZ : (xs + 1) * lats * NZ, :] = both
            for t in range(NZ):
                send2[chunk, t] = fold[pl.ds(t, zlats, stride=NZ), :].astype(BF16)

            if chunk == 0:

                @pl.when(lev == 1)
                def _():
                    pl.semaphore_wait(told, 1)

            mine = pl.ds(pl.multiple_of(lev * side + z * zlats, 8), zlats)

            def go2(t):
                to = ring(t)
                send(
                    send2.at[chunk, to], table_in.at[l, mine], s2.at[i], r2.at[l],
                    dev(yl, to, x, par, i),
                )

            loop(0, NZ - 1, go2)
            post(
                lev == i, send2.at[chunk, z], table_in.at[l, mine], s2.at[i], r2.at[l],
                (w, par, i),
            )
            if chunk == 0:

                @pl.when(lev == 0)
                def _():
                    pl.semaphore_wait(turn, 1)
                    go1(1, 2, 2)

        get_leg.wait()
        swap.wait_recv()
        for l in range(2):
            await_bytes(table_in.at[l], r2.at[l])
            for b in range(nlat // 256):
                turned[l * half : (l + 1) * half, b * 256 : (b + 1) * 256] = dot(
                    eye[:half, :half], table_in[l, b * 256 : (b + 1) * 256, :], ((1,), (1,))
                ).astype(BF16)
        wave = slots_s[2 * w + lev]

        def mix(index, value):
            high = value.astype(BF16)
            low = (value - high.astype(F32)).astype(BF16)
            return dot(modes[index], jnp.concatenate([high, low, high], axis=0))

        for start in range(0, degrees, 256):
            raw = dot(turned[...], table[:, start : start + 256])
            k = lax.broadcasted_iota(jnp.int32, (1, 256), 1) + start
            n = wave + 2 * k + par
            kept = jnp.where(n <= top, raw, 0.0)
            nf = n.astype(F32)
            stiff = nf * (nf + 1.0) / (top * (top + 1.0))
            damped = mix(0, kept) / (1.0 + stiff * rates_col)
            new = mix(1, damped).astype(BF16)
            updated[start : start + 256, :] = dot(eye, new, ((1,), (1,))).astype(BF16)

        kept_half = degrees // 2
        lanes = pl.ds(pl.multiple_of(lev * width, width), width)
        put_spec = pltpu.make_async_copy(
            updated.at[pl.ds(lev * kept_half, kept_half)], spectral.at[0, :, lanes], spec_sem.at[0]
        )
        put_spec.start()

        for start in range(0, nlat, 256):
            new = dot(table[start : start + 256, :], updated[...]).astype(BF16)
            for l in range(2):
                parts[l, start : start + 256, :] = new[:, l * half : (l + 1) * half]

        for l in range(2):

            here = (lev * 2 + l) * NZ + z

            def rows_of(y, zz):
                return parts.at[l, pl.ds(pl.multiple_of(y * side + zz * zlats, 8), zlats)]

            def go3(t):
                to = ring(t)
                for y in range(2):
                    send(
                        rows_of(y, to), recv3.at[here], s3.at[0], r3.at[lev * 2 + l],
                        dev(yl, to, x, par, y),
                    )

            loop(0, NZ - 1, go3)
            send(
                rows_of(1 - lev, z), recv3.at[here], s3.at[0], r3.at[lev * 2 + l],
                (w, par, 1 - lev),
            )
            pltpu.make_async_copy(rows_of(lev, z), recv3.at[here], r3.at[lev * 2 + l]).start()

        swap_spec = pltpu.make_async_remote_copy(
            src_ref=updated.at[pl.ds((1 - lev) * kept_half, kept_half)],
            dst_ref=spectral.at[0, :, lanes],
            send_sem=spec_send.at[0], recv_sem=spec_recv.at[0],
            device_id=(w, par, 1 - lev), device_id_type=MESH,
        )
        swap_spec.start()

        for chunk in range(4):
            i, l = chunk // 2, chunk % 2
            await_bytes(recv3.at[pl.ds(chunk * NZ, NZ)], r3.at[chunk])
            for t in range(NZ):
                fold[t * zlats : (t + 1) * zlats, :] = recv3[chunk * NZ + t].astype(F32)
            for lat in range(zlats):
                picked = fold[pl.ds(lat, NZ, stride=zlats), :]
                send4[chunk, lat // lats, lat % lats] = picked.astype(BF16)

            def go4(n):
                xx, d = plane_src(n, l)
                send(
                    send4.at[chunk, xx], recv4.at[i, par * peers + (yl << 2) + x],
                    s4.at[i], r4.at[i], d,
                )

            loop(0, 4, go4)
            loop(5, 8, go4)
            xx, d = plane_src(4, l)
            post(
                local & (lev == l), send4.at[chunk, xx],
                recv4.at[i, par * peers + (yl << 2) + x], s4.at[i], r4.at[i], d,
            )

        for i in range(2):
            await_bytes(recv4.at[i], r4.at[i])
            for pair in range(lats // 2):
                cols = [recv4[i, :, 2 * pair + b].reshape(2 * rows, half) for b in range(2)]
                share = dot(
                    back[:, 2 * i * rows : 2 * (i + 1) * rows], jnp.concatenate(cols, axis=1)
                )
                if i == 0:
                    early[pair] = share
                else:
                    both = (early[pair] + share).astype(BF16)
                    for b in range(2):
                        columns[0, 2 * pair + b] = both[:, b * half : (b + 1) * half]

        swap.wait_send()
        swap_spec.wait()
        put_spec.wait()
        await_bytes(recv3.at[pl.ds(0, 2 * NZ * CORES - 2)], s3.at[0])

        def drain(ref, count, sem, has_local):
            @pl.when(has_local)
            def _():
                await_bytes(ref.at[pl.ds(0, count - 1)], sem)

            @pl.when(jnp.logical_not(has_local))
            def _():
                await_bytes(ref.at[pl.ds(0, count)], sem)

        drain(recv1.at[0], peers, s1.at[1], local)
        drain(recv1.at[1], 2 * peers, s1.at[2], local)
        for i in range(2):
            drain(recv4.at[i], 2 * peers, s4.at[i], local)

            @pl.when(lev == i)
            def _():
                await_bytes(recv3.at[pl.ds(0, 2 * NZ - 2)], s2.at[i])

            @pl.when(lev != i)
            def _():
                await_bytes(recv3.at[pl.ds(0, 2 * NZ)], s2.at[i])

    scratch = [
        pltpu.SMEM((lats,), F32),
        pltpu.SMEM((waves,), jnp.int32),
        pltpu.VMEM((1, waves), jnp.int32),
        pltpu.VMEM((half, half), F32),
        pltpu.VMEM((half, half), F32),
        pltpu.VMEM((1, half), F32),
        pltpu.VMEM((lats, waves, half), BF16),
        pltpu.VMEM((2, peers, lats, NZ, half), BF16),
        pltpu.VMEM((2, 2 * peers, lats, NZ, half), BF16),
        pltpu.VMEM((zlats * NZ, half), F32),
        pltpu.VMEM((4, NZ, zlats, half), BF16),
        pltpu.VMEM((2, nlat, half), BF16),
        pltpu.VMEM((nlat, degrees), BF16),
        pltpu.VMEM((2, width, 3 * width), BF16),
        pltpu.VMEM((waves, waves), BF16),
        pltpu.VMEM((waves, 2 * waves), BF16),
        pltpu.VMEM((degrees, width), BF16),
        pltpu.VMEM((2, nlat, half), BF16),
        pltpu.VMEM((4 * NZ, zlats, half), BF16),
        pltpu.VMEM((4, NX, lats, NZ, half), BF16),
        pltpu.VMEM((2, 2 * peers, lats, NZ, half), BF16),
        pltpu.VMEM((width, nlat), BF16),
        pltpu.VMEM((lats // 2, waves, 2 * half), F32),
        pltpu.SemaphoreType.DMA((2,)),
        pltpu.SemaphoreType.DMA((6,)),
    ] + [pltpu.SemaphoreType.DMA((1,))] * 5 + [
        pltpu.SemaphoreType.DMA((3,)),
        pltpu.SemaphoreType.DMA((4,)),
        pltpu.SemaphoreType.DMA((2,)),
        pltpu.SemaphoreType.DMA((2,)),
        pltpu.SemaphoreType.DMA((1,)),
        pltpu.SemaphoreType.DMA((4,)),
        pltpu.SemaphoreType.DMA((2,)),
        pltpu.SemaphoreType.DMA((2,)),
        pltpu.SemaphoreType.REGULAR,
        pltpu.SemaphoreType.REGULAR((2,)),
        pltpu.SemaphoreType.REGULAR,
    ]
    return kernel, scratch


def per_device(fourier, legendre, quad_weights, slot_wave, to_modes, from_modes, mode_rates):
    _, lats, waves, half = fourier.shape
    degrees = legendre.shape[3]
    kernel, scratch = make_kernel(lats, waves, half, degrees)
    vmem = pl.BlockSpec(memory_space=pltpu.VMEM)
    hbm = pl.BlockSpec(memory_space=pltpu.HBM)
    operands = (
        fourier, legendre, quad_weights, slot_wave, slot_wave.reshape(1, waves),
        to_modes, from_modes, mode_rates.reshape(1, half),
    )
    return pl.pallas_call(
        kernel,
        out_shape=(
            jax.ShapeDtypeStruct(fourier.shape, BF16),
            jax.ShapeDtypeStruct((1, degrees // 2, 2 * 2 * half), BF16),
        ),
        in_specs=[hbm] * 8,
        out_specs=(vmem, vmem),
        scratch_shapes=scratch,
        compiler_params=pltpu.CompilerParams(
            collective_id=0, has_side_effects=True, vmem_limit_bytes=48 * 2**20
        ),
    )(*[pltpu.with_memory_space_constraint(v, pltpu.HBM) for v in operands])


def solution(mesh):
    in_specs = (
        P("parity", "wave", None, "lev"),
        P("wave", "parity", "lev", None),
        P("wave"),
        P(),
        P(),
        P(),
        P(),
    )
    out_specs = (P("parity", "wave", None, "lev"), P("parity", "lev", "wave"))
    return jax.shard_map(
        per_device, mesh=mesh, in_specs=in_specs, out_specs=out_specs, check_vma=False
    )
```

```python
import jax
import jax.numpy as jnp
from jax import lax
from jax.experimental import pallas as pl
from jax.experimental.pallas import tpu as pltpu
from jax.sharding import PartitionSpec as P

MESH = pl.DeviceIdType.MESH
F32 = jnp.float32
BF16 = jnp.bfloat16
NY, NZ, NX = 2, 16, 4
CORES = 2


def dot(a, b, dims=((1,), (0,)), precision=None):
    return lax.dot_general(a, b, (dims, ((), ())), precision=precision, preferred_element_type=F32)


def make_kernel(lats, waves, half, degrees):
    nlat = NY * NZ * NX * lats
    zlats = NX * lats
    side = nlat // 2
    width = 2 * half
    peers = NY * NX
    rows = waves // 2
    top = 2 * degrees - 1

    def kernel(
        fourier, legendre, quad_in, slots_in, slots_row, to_in, from_in, rates_in,
        columns, spectral,
        quad, slots_s, slots_v, to_modes, from_modes, rates,
        grid_in, send1, recv1, fold, send2, table_in, table, modes, picks, back,
        updated, parts, recv3, send4, recv4, turned, early,
        local_sem, small_sem, bar_leg, leg_send, spec_sem, spec_send, spec_recv,
        s1, r1, s2, r2, s3, r3, s4, r4, turn, known, told,
    ):
        w = lax.axis_index("wave")
        par = lax.axis_index("parity")
        lev = lax.axis_index("lev")
        yl = w >> 6
        z = (w >> 2) & 15
        x = w & 3
        local = lev == yl
        sign = (1 - 2 * par).astype(F32)

        def dev(y, zz, xx, q, l):
            return ((y << 6) + (zz << 2) + xx, q, l)

        def plane_dst(n):
            q = (par + 1 + (n >> 3)) & 1
            y = (yl + (n >> 2)) & 1
            xx = (x + n * (1 - 2 * lev)) & 3
            return (y << 2) + xx, dev(y, z, xx, q, yl)

        def plane_src(n, l):
            h = (par + 1 + (n >> 2)) & 1
            xx = (x + n * (1 - 2 * lev)) & 3
            return xx, dev(lev, z, xx, h, l)

        def ring(t):
            away = ((t + 1) >> 1) * ((2 * (t & 1) - 1) * (1 - 2 * lev))
            return (z + 8 + away) & 15

        def signal(d, sem):
            pl.semaphore_signal(sem, inc=1, device_id=d, device_id_type=MESH)

        def send(src, dst, send_sem, recv_sem, d):
            pltpu.make_async_remote_copy(
                src_ref=src, dst_ref=dst, send_sem=send_sem, recv_sem=recv_sem,
                device_id=d, device_id_type=MESH,
            ).start()

        def post(me, src, dst, send_sem, recv_sem, d):
            @pl.when(jnp.logical_not(me))
            def _():
                send(src, dst, send_sem, recv_sem, d)

            @pl.when(me)
            def _():
                pltpu.make_async_copy(src, dst, recv_sem).start()

        def loop(first, last, body):
            def step(n, _):
                body(n)
                return 0

            lax.fori_loop(first, last, step, 0)

        def await_bytes(ref, sem):
            pltpu.make_async_copy(ref, ref, sem).wait()

        get_grid = pltpu.make_async_copy(fourier.at[0], grid_in, local_sem.at[0])
        get_grid.start()
        small = [
            pltpu.make_async_copy(src, dst, small_sem.at[n])
            for n, (src, dst) in enumerate((
                (slots_row, slots_v), (quad_in, quad), (slots_in, slots_s),
                (to_in, to_modes), (from_in, from_modes), (rates_in, rates),
            ))
        ]
        for copy in small[:2]:
            copy.start()

        barrier = pltpu.get_barrier_semaphore()

        def tell(away, sem):
            for side_to in (-away, away):
                signal(dev(yl, (z + side_to) & 15, x, par, 0), sem)

        tell(1, barrier)
        tell(2, barrier)

        def greet_dst(n):
            signal(plane_dst(n)[1], barrier)

        def greet_src(n):
            for l in range(2):
                signal(plane_src(n, l)[1], barrier)

        loop(0, 8, greet_dst)
        loop(9, 16, greet_dst)
        loop(0, 4, greet_src)
        loop(5, 8, greet_src)
        signal((w, par, 1 - lev), barrier)
        signal(plane_src(4, 1 - lev)[1], barrier)

        @pl.when(jnp.logical_not(local))
        def _():
            signal(plane_dst(8)[1], barrier)
            signal(plane_src(4, lev)[1], barrier)

        get_leg = pltpu.make_async_copy(
            legendre.at[lev, 0], table.at[pl.ds(lev * side, side)], local_sem.at[1]
        )
        get_leg.start()
        for copy in small[2:]:
            copy.start()

        small[0].wait()
        small[1].wait()

        row = lax.broadcasted_iota(jnp.int32, (waves, waves), 0)
        col = lax.broadcasted_iota(jnp.int32, (waves, waves), 1)
        hot = (row == slots_v[...]).astype(F32).astype(BF16)
        zz = row & 15
        xx = (row >> 4) & 3
        yy = (row >> 6) & 1
        ii = row >> 7
        order = (col == (((yy * NZ + zz) * NX + xx) * 2 + ii)).astype(F32).astype(BF16)
        picks[...] = dot(order, hot, ((1,), (1,))).astype(BF16)

        def permute(i):
            for pair in range(lats // 2):
                both = jnp.concatenate([grid_in[2 * pair + b] for b in range(2)], axis=1)
                moved = dot(picks[i * rows : (i + 1) * rows, :], both).astype(BF16)
                for b in range(2):
                    block = moved[:, b * half : (b + 1) * half]
                    send1[i, :, 2 * pair + b] = block.reshape(peers, NZ, half)

        get_grid.wait()
        for lat in range(lats):
            grid_in[lat] = (quad[lat] * grid_in[lat].astype(F32)).astype(BF16)
        permute(0)

        different = (lev != yl).astype(jnp.int32)
        first = (lev == 0).astype(jnp.int32)
        pl.semaphore_wait(barrier, 2 * (2 * peers - 1) + 1 + 2 * different + 8 * first)

        def go1(i, far, near):
            def parts_of(n):
                p, d = plane_dst(n)
                return send1.at[i, p], recv1.at[i, lev * peers + par * NX + x], d

            def one(sem):
                def body(n):
                    src, dst, d = parts_of(n)
                    send(src, dst, s1.at[sem], r1.at[i * 2 + lev], d)

                return body

            loop(0, 8, one(far))
            loop(9, 16, one(near))
            src, dst, d = parts_of(8)
            post(local, src, dst, s1.at[near], r1.at[i * 2 + lev], d)

        def pass_on():
            await_bytes(recv1.at[0, pl.ds(0, peers)], s1.at[0])
            signal((w, par, 1 - lev), turn)

        @pl.when(lev == 0)
        def _():
            tell(2, known.at[0])
            go1(0, 0, 1)
            pl.semaphore_wait(known.at[0], 2)
            tell(4, known.at[1])

        permute(1)

        @pl.when(lev == 0)
        def _():
            pass_on()
            pl.semaphore_wait(known.at[1], 2)
            signal((w, par, 1), told)

        @pl.when(lev == 1)
        def _():
            pl.semaphore_wait(turn, 1)
            go1(0, 0, 1)
            go1(1, 2, 2)
            pass_on()

        swap = pltpu.make_async_remote_copy(
            src_ref=legendre.at[1 - lev, 0],
            dst_ref=table.at[pl.ds(lev * side, side)],
            send_sem=leg_send.at[0], recv_sem=bar_leg.at[0],
            device_id=(w, par, 1 - lev), device_id_type=MESH,
        )
        swap.start()

        for copy in small[2:]:
            copy.wait()

        into = dot(hot, order, ((1,), (1,)))
        for i in range(2):
            one = into[:, i * rows : (i + 1) * rows]
            back[:, (2 * i) * rows : (2 * i + 1) * rows] = one.astype(BF16)
            back[:, (2 * i + 1) * rows : (2 * i + 2) * rows] = (sign * one).astype(BF16)

        wide_l = lax.broadcasted_iota(jnp.int32, (width, half), 0) >> 1
        spread = (wide_l == lax.broadcasted_iota(jnp.int32, (width, half), 1)).astype(F32)
        same = ((row ^ col) & 1) == 0
        for index, square in enumerate((to_modes, from_modes)):
            tall = dot(spread, square[...], precision=lax.Precision.HIGHEST)
            full = dot(tall, spread, ((1,), (1,)), precision=lax.Precision.HIGHEST)
            full = jnp.where(same, full, 0.0)
            high = full.astype(BF16)
            low = (full - high.astype(F32)).astype(BF16)
            modes[index] = jnp.concatenate([high, high, low], axis=1)
        rates_col = jnp.sum(spread * rates[...], axis=1, keepdims=True)
        eye = (row == col).astype(F32).astype(BF16)

        for chunk in range(4):
            i, l = chunk // 2, chunk % 2
            await_bytes(recv1.at[i, pl.ds(l * peers, peers)], r1.at[chunk])
            for xs in range(NX):
                north = recv1[i, l * peers + xs].astype(F32)
                south = recv1[i, l * peers + NX + xs].astype(F32)
                both = (north + sign * south).reshape(lats * NZ, half)
                fold[xs * lats * NZ : (xs + 1) * lats * NZ, :] = both
            for t in range(NZ):
                send2[chunk, t] = fold[pl.ds(t, zlats, stride=NZ), :].astype(BF16)

            if chunk == 0:

                @pl.when(lev == 1)
                def _():
                    pl.semaphore_wait(told, 1)

            mine = pl.ds(pl.multiple_of(lev * side + z * zlats, 8), zlats)

            def go2(t):
                to = ring(t)
                send(
                    send2.at[chunk, to], table_in.at[l, mine], s2.at[i], r2.at[l],
                    dev(yl, to, x, par, i),
                )

            loop(0, NZ - 1, go2)
            post(
                lev == i, send2.at[chunk, z], table_in.at[l, mine], s2.at[i], r2.at[l],
                (w, par, i),
            )
            if chunk == 0:

                @pl.when(lev == 0)
                def _():
                    pl.semaphore_wait(turn, 1)
                    go1(1, 2, 2)

        get_leg.wait()
        swap.wait_recv()
        for l in range(2):
            await_bytes(table_in.at[l], r2.at[l])
            for b in range(nlat // 256):
                turned[l * half : (l + 1) * half, b * 256 : (b + 1) * 256] = dot(
                    eye[:half, :half], table_in[l, b * 256 : (b + 1) * 256, :], ((1,), (1,))
                ).astype(BF16)
        wave = slots_s[2 * w + lev]

        def mix(index, value):
            high = value.astype(BF16)
            low = (value - high.astype(F32)).astype(BF16)
            return dot(modes[index], jnp.concatenate([high, low, high], axis=0))

        for start in range(0, degrees, 256):
            raw = dot(turned[...], table[:, start : start + 256])
            k = lax.broadcasted_iota(jnp.int32, (1, 256), 1) + start
            n = wave + 2 * k + par
            kept = jnp.where(n <= top, raw, 0.0)
            nf = n.astype(F32)
            stiff = nf * (nf + 1.0) / (top * (top + 1.0))
            damped = mix(0, kept) / (1.0 + stiff * rates_col)
            new = mix(1, damped).astype(BF16)
            updated[start : start + 256, :] = dot(eye, new, ((1,), (1,))).astype(BF16)

        kept_half = degrees // 2
        lanes = pl.ds(pl.multiple_of(lev * width, width), width)
        put_spec = pltpu.make_async_copy(
            updated.at[pl.ds(lev * kept_half, kept_half)], spectral.at[0, :, lanes], spec_sem.at[0]
        )
        put_spec.start()

        def rows_of(l, y, zz):
            return parts.at[l, pl.ds(pl.multiple_of(y * side + zz * zlats, 8), zlats)]

        def give(l, y):
            here = recv3.at[(lev * 2 + l) * NZ + z]
            arrived = r3.at[lev * 2 + l]

            def go3(t):
                to = ring(t)
                send(rows_of(l, y, to), here, s3.at[0], arrived, dev(yl, to, x, par, y))

            loop(0, NZ - 1, go3)
            post(lev == y, rows_of(l, y, z), here, s3.at[0], arrived, (w, par, y))

        for y in range(2):
            for start in range(y * side, (y + 1) * side, side // 2):
                new = dot(table[start : start + side // 2, :], updated[...]).astype(BF16)
                for l in range(2):
                    parts[l, start : start + side // 2, :] = new[:, l * half : (l + 1) * half]
            give(0, y)
        for y in range(2):
            give(1, y)

        swap_spec = pltpu.make_async_remote_copy(
            src_ref=updated.at[pl.ds((1 - lev) * kept_half, kept_half)],
            dst_ref=spectral.at[0, :, lanes],
            send_sem=spec_send.at[0], recv_sem=spec_recv.at[0],
            device_id=(w, par, 1 - lev), device_id_type=MESH,
        )
        swap_spec.start()

        for chunk in range(4):
            i, l = chunk // 2, chunk % 2
            await_bytes(recv3.at[pl.ds(chunk * NZ, NZ)], r3.at[chunk])
            for t in range(NZ):
                fold[t * zlats : (t + 1) * zlats, :] = recv3[chunk * NZ + t].astype(F32)
            for lat in range(zlats):
                picked = fold[pl.ds(lat, NZ, stride=zlats), :]
                send4[chunk, lat // lats, lat % lats] = picked.astype(BF16)

            def go4(n):
                xx, d = plane_src(n, l)
                send(
                    send4.at[chunk, xx], recv4.at[i, par * peers + (yl << 2) + x],
                    s4.at[i], r4.at[i], d,
                )

            loop(0, 4, go4)
            loop(5, 8, go4)
            xx, d = plane_src(4, l)
            post(
                local & (lev == l), send4.at[chunk, xx],
                recv4.at[i, par * peers + (yl << 2) + x], s4.at[i], r4.at[i], d,
            )

        for i in range(2):
            await_bytes(recv4.at[i], r4.at[i])
            for pair in range(lats // 2):
                cols = [recv4[i, :, 2 * pair + b].reshape(2 * rows, half) for b in range(2)]
                share = dot(
                    back[:, 2 * i * rows : 2 * (i + 1) * rows], jnp.concatenate(cols, axis=1)
                )
                if i == 0:
                    early[pair] = share
                else:
                    both = (early[pair] + share).astype(BF16)
                    for b in range(2):
                        columns[0, 2 * pair + b] = both[:, b * half : (b + 1) * half]

        swap.wait_send()
        swap_spec.wait()
        put_spec.wait()
        await_bytes(recv3.at[pl.ds(0, 2 * NZ * CORES - 2)], s3.at[0])

        def drain(ref, count, sem, has_local):
            @pl.when(has_local)
            def _():
                await_bytes(ref.at[pl.ds(0, count - 1)], sem)

            @pl.when(jnp.logical_not(has_local))
            def _():
                await_bytes(ref.at[pl.ds(0, count)], sem)

        drain(recv1.at[0], peers, s1.at[1], local)
        drain(recv1.at[1], 2 * peers, s1.at[2], local)
        for i in range(2):
            drain(recv4.at[i], 2 * peers, s4.at[i], local)

            @pl.when(lev == i)
            def _():
                await_bytes(recv3.at[pl.ds(0, 2 * NZ - 2)], s2.at[i])

            @pl.when(lev != i)
            def _():
                await_bytes(recv3.at[pl.ds(0, 2 * NZ)], s2.at[i])

    scratch = [
        pltpu.SMEM((lats,), F32),
        pltpu.SMEM((waves,), jnp.int32),
        pltpu.VMEM((1, waves), jnp.int32),
        pltpu.VMEM((half, half), F32),
        pltpu.VMEM((half, half), F32),
        pltpu.VMEM((1, half), F32),
        pltpu.VMEM((lats, waves, half), BF16),
        pltpu.VMEM((2, peers, lats, NZ, half), BF16),
        pltpu.VMEM((2, 2 * peers, lats, NZ, half), BF16),
        pltpu.VMEM((zlats * NZ, half), F32),
        pltpu.VMEM((4, NZ, zlats, half), BF16),
        pltpu.VMEM((2, nlat, half), BF16),
        pltpu.VMEM((nlat, degrees), BF16),
        pltpu.VMEM((2, width, 3 * width), BF16),
        pltpu.VMEM((waves, waves), BF16),
        pltpu.VMEM((waves, 2 * waves), BF16),
        pltpu.VMEM((degrees, width), BF16),
        pltpu.VMEM((2, nlat, half), BF16),
        pltpu.VMEM((4 * NZ, zlats, half), BF16),
        pltpu.VMEM((4, NX, lats, NZ, half), BF16),
        pltpu.VMEM((2, 2 * peers, lats, NZ, half), BF16),
        pltpu.VMEM((width, nlat), BF16),
        pltpu.VMEM((lats // 2, waves, 2 * half), F32),
        pltpu.SemaphoreType.DMA((2,)),
        pltpu.SemaphoreType.DMA((6,)),
    ] + [pltpu.SemaphoreType.DMA((1,))] * 5 + [
        pltpu.SemaphoreType.DMA((3,)),
        pltpu.SemaphoreType.DMA((4,)),
        pltpu.SemaphoreType.DMA((2,)),
        pltpu.SemaphoreType.DMA((2,)),
        pltpu.SemaphoreType.DMA((1,)),
        pltpu.SemaphoreType.DMA((4,)),
        pltpu.SemaphoreType.DMA((2,)),
        pltpu.SemaphoreType.DMA((2,)),
        pltpu.SemaphoreType.REGULAR,
        pltpu.SemaphoreType.REGULAR((2,)),
        pltpu.SemaphoreType.REGULAR,
    ]
    return kernel, scratch


def per_device(fourier, legendre, quad_weights, slot_wave, to_modes, from_modes, mode_rates):
    _, lats, waves, half = fourier.shape
    degrees = legendre.shape[3]
    kernel, scratch = make_kernel(lats, waves, half, degrees)
    vmem = pl.BlockSpec(memory_space=pltpu.VMEM)
    hbm = pl.BlockSpec(memory_space=pltpu.HBM)
    operands = (
        fourier, legendre, quad_weights, slot_wave, slot_wave.reshape(1, waves),
        to_modes, from_modes, mode_rates.reshape(1, half),
    )
    return pl.pallas_call(
        kernel,
        out_shape=(
            jax.ShapeDtypeStruct(fourier.shape, BF16),
            jax.ShapeDtypeStruct((1, degrees // 2, 2 * 2 * half), BF16),
        ),
        in_specs=[hbm] * 8,
        out_specs=(vmem, vmem),
        scratch_shapes=scratch,
        compiler_params=pltpu.CompilerParams(
            collective_id=0, has_side_effects=True, vmem_limit_bytes=48 * 2**20
        ),
    )(*[pltpu.with_memory_space_constraint(v, pltpu.HBM) for v in operands])


def solution(mesh):
    in_specs = (
        P("parity", "wave", None, "lev"),
        P("wave", "parity", "lev", None),
        P("wave"),
        P(),
        P(),
        P(),
        P(),
    )
    out_specs = (P("parity", "wave", None, "lev"), P("parity", "lev", "wave"))
    return jax.shard_map(
        per_device, mesh=mesh, in_specs=in_specs, out_specs=out_specs, check_vma=False
    )
```
